512 devices in a mesh: sub: 16 (over x_lo, y), elem: 32 (over z, x_hi, core).
Axes of the slice: x: 4 (x_hi: 2, x_lo: 2; x = x_hi * 2 + x_lo), y: 8, z: 8, core: 2. Of those that a mesh axis runs over, the one named last changes fastest.
Arguments:
- element_tiles: bfloat16 [4096, 128, 128], P(('sub', 'elem')), parts along dimension 0, may hold values from -0.5 to 0.5
- element_blocks: int32 [4096, 2], P(('sub', 'elem')), parts along dimension 0, may hold values from 0 to 31
- mode_shapes: bfloat16 [65536, 1024], P(('sub', 'elem')), parts along dimension 0, may hold values from -0.5 to 0.5
- trial_modes: bfloat16 [16384, 128], P('sub'), parts along dimension 0, may hold values from -0.1875 to 0.1875
Outputs:
- reduced_stiffness: float32 [16384, 1024], P(('sub', 'elem')), parts along dimension 0
- interface_forces: float32 [16384, 128], P(('sub', 'elem')), parts along dimension 0
The draws below stay inside these ranges and needn't reach their ends.
There are 16 independent parts, one for each index of `sub`. The reference program is written for one: setup_inputs(seed, part) draws one part's arguments, and reference() takes and returns one part's arrays. A program takes and returns all parts, laid end to end along the dimension named above; each array names one. Nothing has to cross between parts.
Inputs may be any that keep to these rules, and one draw needn't show every extreme that they name: `element_blocks`: each row gives the row block and the column block of one element tile.
All inputs are finite; a program needn't handle non-finite values.
Results may differ from the reference program's by a relative error of at most 0.0029.
Values may be sent and summed in bfloat16 or wider, within the bound.
A program may use at most 64 MiB of HBM per device.

```python
import jax
import jax.numpy as jnp
from jax import lax

NI = 4096
M = 1024
BLOCK = 128
NRHS = 128
ELEMS = 256
NB = 32


def place_ends(result, key, low, largest):
    spot = [jax.random.randint(jax.random.fold_in(key, axis), (), 0, length) for axis, length in enumerate(result.shape)]
    main_axis = result.shape.index(max(result.shape))
    beside = spot[:main_axis] + [(spot[main_axis] + 1) % result.shape[main_axis]] + spot[main_axis + 1:]
    return result.at[tuple(spot)].set(low).at[tuple(beside)].set(largest)


def block_levels(stream_key, dims, cuts, low, high):
    def one(dim, parts):
        draws = jax.random.uniform(jax.random.fold_in(jax.random.fold_in(stream_key, 6), dim), (parts,), jnp.float32, low / len(cuts), high / len(cuts))
        return jnp.repeat(jnp.exp(draws), dims[dim] // parts).reshape((-1,) + (1,) * (len(dims) - dim - 1))

    level = one(*cuts[0])
    for cut in cuts[1:]:
        level = level * one(*cut)
    return level


def centred(rng, dims, width, bound, cuts=(), kind=jnp.bfloat16):
    level = block_levels(rng, dims, cuts, -0.22, 0.18) if cuts else 1.0
    result = jax.random.normal(rng, dims, jnp.float32) * width * level
    return jnp.minimum(jnp.maximum(result, -bound), bound).astype(kind)


def setup_inputs(seed: int = 0, part: int = 0) -> dict:
    key_of = jax.random.split(jax.random.key(seed), 5)
    own_keys = jax.random.split(jax.random.fold_in(key_of[4], part), 5)
    return {
        "element_tiles": centred(own_keys[0], (ELEMS, BLOCK, BLOCK), BLOCK ** -0.5, 0.5, ((0, 32),)),
        "element_blocks": place_ends(jax.random.randint(own_keys[1], (ELEMS, 2), 0, NB), jax.random.fold_in(own_keys[1], 1), 0, NB - 1).astype(jnp.int32),
        "mode_shapes": centred(own_keys[2], (NI, M), BLOCK ** -0.5, 0.5, ((0, 32),)),
        "trial_modes": centred(own_keys[3], (M, NRHS), M ** -0.5, 0.1875),
    }


def reference(element_tiles, element_blocks, mode_shapes, trial_modes):
    blocks = mode_shapes.reshape(NI // BLOCK, BLOCK, M)
    row_side = jnp.take(blocks, element_blocks[:, 0], axis=0).reshape(-1, M)
    col_side = jnp.take(blocks, element_blocks[:, 1], axis=0)
    stiff_modes = jnp.einsum("eij,ejm->eim", element_tiles.astype(jnp.float32), col_side.astype(jnp.float32))
    stiff_modes = stiff_modes.astype(jnp.bfloat16).reshape(-1, M)
    reduced = lax.dot_general(row_side, stiff_modes, (((0,), (0,)), ((), ())), preferred_element_type=jnp.float32)
    forces = jnp.dot(reduced, trial_modes.astype(jnp.float32), precision=lax.Precision.HIGHEST)
    return reduced, forces
```

```python
import functools

import jax
import jax.numpy as jnp
from jax import lax
from jax.experimental import pallas as pl
from jax.experimental.pallas import tpu as pltpu
from jax.sharding import PartitionSpec as P

MESH = pl.DeviceIdType.MESH
NZ = 8
PIECES = 2


def kernel(tiles, blocks, modes, trial, reduced, forces, pbuf, turned, tbuf, ids, stiff, out_parts, in_parts, tr,
           own_sem, p_send, p_recv, s_recv, t_send, t_recv, i_send, i_recv, r_send, r_recv):
    e = lax.axis_index("elem")
    c = lax.rem(e, 2)
    xh = lax.rem(e // 2, 2)
    z = e // 4
    q = lax.rem(e, 4)
    s = 1 - 2 * c
    rows = modes.shape[0] // PIECES
    per = tiles.shape[0]
    wide = stiff.shape[0]

    def rank(dz, other_x=False, other_c=False):
        level = lax.rem(z + dz + 2 * NZ, NZ)
        return level * 4 + 2 * (1 - xh if other_x else xh) + (1 - c if other_c else c)

    ahead, behind, across, beside = rank(s), rank(-s), rank(0, True), rank(0, False, True)
    barrier = pltpu.get_barrier_semaphore()
    for device in (ahead, behind, across, beside):
        pl.semaphore_signal(barrier, inc=1, device_id={"elem": device}, device_id_type=MESH)
    pl.semaphore_wait(barrier, 4)

    waits = []

    def put(src, dst, send, recv, device):
        copy = pltpu.make_async_remote_copy(
            src_ref=src, dst_ref=dst, send_sem=send, recv_sem=recv, device_id={"elem": device}, device_id_type=MESH
        )
        copy.start()
        waits.append(copy)

    counter = [0]

    def send_piece(src, block, p, slot, device, beside_slot=None):
        n = counter[0]
        counter[0] += 1
        dst = pbuf.at[block, pl.ds(p * rows, rows)]
        recv = p_recv.at[slot, p] if beside_slot is None else s_recv.at[beside_slot, p]
        put(src, dst, p_send.at[n], recv, device)

    block_of = {}
    for j in range(1, 5):
        block_of[j - 1] = rank(-j * s)
    for j in range(1, 4):
        block_of[3 + j] = rank(j * s)
    for j in range(0, 5):
        block_of[7 + j] = rank(-j * s, True)
    for j in range(1, 4):
        block_of[11 + j] = rank(j * s, True)
    block_of[15] = e

    def arrived(slot, p):
        part = pbuf.at[block_of[slot], pl.ds(p * rows, rows)]
        pltpu.make_async_remote_copy(
            src_ref=part, dst_ref=part, send_sem=p_send.at[0], recv_sem=p_recv.at[slot, p],
            device_id={"elem": e}, device_id_type=MESH,
        ).wait_recv()
        return part

    keep = pltpu.make_async_copy(modes, pbuf.at[e], own_sem.at[0])
    keep.start()
    for p in range(PIECES):
        part = modes.at[pl.ds(p * rows, rows)]
        send_piece(part, e, p, 0, ahead)
        send_piece(part, e, p, 7, across)
        send_piece(part, e, p, 4, behind)
    for p in range(PIECES):
        send_piece(modes.at[pl.ds(p * rows, rows)], e, p, None, beside, 15)
    put(blocks, ids.at[1], i_send.at[0], i_recv.at[0], beside)
    put(blocks, ids.at[2], i_send.at[1], i_recv.at[1], across)
    put(tiles, tbuf.at[1], t_send.at[0], t_recv.at[0], beside)
    put(tiles, tbuf.at[2], t_send.at[1], t_recv.at[1], across)
    keep_t = pltpu.make_async_copy(tiles, tbuf.at[0], own_sem.at[1])
    keep_t.start()
    keep_i = pltpu.make_async_copy(blocks, ids.at[0], own_sem.at[2])
    keep_i.start()
    keep_r = pltpu.make_async_copy(trial, tr, own_sem.at[3])
    keep_r.start()

    for r in range(5):
        for p in range(PIECES):
            if r + 1 <= 4:
                part = arrived(r, p)
                if r + 1 < 4:
                    send_piece(part, block_of[r], p, r + 1, ahead)
                send_piece(part, block_of[r], p, None, beside, r)
            part = arrived(7 + r, p)
            if r < 4:
                send_piece(part, block_of[7 + r], p, 8 + r, ahead)
            send_piece(part, block_of[7 + r], p, None, beside, 7 + r)
            if r + 1 <= 3:
                part = arrived(4 + r, p)
                if r + 1 < 3:
                    send_piece(part, block_of[4 + r], p, 5 + r, behind)
                send_piece(part, block_of[4 + r], p, 12 + r, across)
                send_piece(part, block_of[4 + r], p, None, beside, 4 + r)
            if 1 <= r <= 3:
                part = arrived(11 + r, p)
                send_piece(part, block_of[11 + r], p, None, beside, 11 + r)
        if r == 1:
            pltpu.make_async_copy(tbuf.at[2], tbuf.at[2], t_recv.at[1]).wait()
            put(tbuf.at[2], tbuf.at[3], t_send.at[2], t_recv.at[2], beside)
            pltpu.make_async_copy(ids.at[2], ids.at[2], i_recv.at[1]).wait()
            put(ids.at[2], ids.at[3], i_send.at[2], i_recv.at[2], beside)
    for slot in range(16):
        block = block_of[slot]
        other = lax.rem(block, 2)
        level = block // 4
        mirrored = lax.rem(2 * z - level + 2 * NZ, NZ)
        theirs = mirrored * 4 + 2 * lax.rem(block // 2, 2) + 1 - other
        for p in range(PIECES):
            part = pbuf.at[theirs, pl.ds(p * rows, rows)]
            pltpu.make_async_copy(part, part, s_recv.at[slot, p]).wait()
    keep.wait()
    keep_t.wait()
    keep_i.wait()
    for k, (sem_t, sem_i) in enumerate(((0, 0), (2, 2))):
        slot = 1 + 2 * k
        pltpu.make_async_copy(tbuf.at[slot], tbuf.at[slot], t_recv.at[sem_t]).wait()
        pltpu.make_async_copy(ids.at[slot], ids.at[slot], i_recv.at[sem_i]).wait()

    cols = pl.ds(pl.multiple_of(q * wide, wide), wide)

    @pl.loop(0, NZ * 4)
    def _(b):
        turned[b] = pbuf[b, :, cols].T

    for g in range(4):
        for i in range(per):
            lhs = turned[ids[g, i, 1]]
            got = lax.dot_general(lhs, tbuf[g, i], (((1,), (1,)), ((), ())), preferred_element_type=jnp.float32)
            k = g * per + i
            stiff[:, k * 128 : (k + 1) * 128] = got.astype(jnp.bfloat16)

    def parts_for(m):
        span = pl.ds(pl.multiple_of(m * 256, 256), 256)
        acc = jnp.zeros((wide, 256), jnp.float32)
        for k in range(0, 4 * per, 2):
            first = pbuf[ids[k // per, k % per, 0], :, span]
            second = pbuf[ids[(k + 1) // per, (k + 1) % per, 0], :, span]
            acc += jnp.dot(
                stiff[:, k * 128 : (k + 2) * 128], jnp.concatenate([first, second], axis=0),
                preferred_element_type=jnp.float32,
            )
        out_parts[span, :] = acc.T.astype(jnp.bfloat16)

    order = (2, 1, 3, 0)
    for n, dm in enumerate(order):
        m = lax.rem(z // 2 + dm, 4)
        parts_for(m)
        for w in range(8):
            if dm == 0:
                target = lax.rem(z, 2) * 4 + q + 1 + w
                target = m * 8 + lax.rem(target, 8)
                if w == 7:
                    in_parts[e] = out_parts[pl.ds(pl.multiple_of(e * 32, 32), 32), :]
                    continue
            else:
                target = m * 8 + w
            k = n * 8 + w
            put(
                out_parts.at[pl.ds(pl.multiple_of(target * 32, 32), 32)], in_parts.at[e],
                r_send.at[k], r_recv.at[e], target,
            )
    for k in range(1, 32):
        source = lax.rem(e + k, 32)
        pltpu.make_async_copy(in_parts.at[source], in_parts.at[source], r_recv.at[source]).wait()
    for quarter in range(4):
        total = jnp.zeros((32, wide), jnp.float32)
        for level in range(NZ):
            total += in_parts[level * 4 + quarter].astype(jnp.float32)
        reduced[:, quarter * wide : (quarter + 1) * wide] = total
    keep_r.wait()
    forces[...] = jnp.dot(
        reduced[...], tr[...].astype(jnp.float32), precision=lax.Precision.HIGHEST, preferred_element_type=jnp.float32
    )
    for copy in waits:
        copy.wait_send()


def body(element_tiles, element_blocks, mode_shapes, trial_modes):
    block, count = mode_shapes.shape
    per = element_tiles.shape[0]
    wide = count // 4
    anywhere = pl.BlockSpec(memory_space=pl.ANY)
    in_vmem = pl.BlockSpec(memory_space=pltpu.VMEM)
    dma = pltpu.SemaphoreType.DMA
    return pl.pallas_call(
        kernel,
        out_shape=(
            jax.ShapeDtypeStruct((count // 32, count), jnp.float32),
            jax.ShapeDtypeStruct((count // 32, trial_modes.shape[1]), jnp.float32),
        ),
        in_specs=[anywhere, pl.BlockSpec(memory_space=pltpu.SMEM), anywhere, anywhere],
        out_specs=(in_vmem, in_vmem),
        scratch_shapes=[
            pltpu.VMEM((NZ * 4, block, count), jnp.bfloat16),
            pltpu.VMEM((NZ * 4, wide, block), jnp.bfloat16),
            pltpu.VMEM((4, per, block, block), jnp.bfloat16),
            pltpu.SMEM((4, per, 2), jnp.int32),
            pltpu.VMEM((wide, 4 * per * block), jnp.bfloat16),
            pltpu.VMEM((count, wide), jnp.bfloat16),
            pltpu.VMEM((NZ * 4, count // 32, wide), jnp.bfloat16),
            pltpu.VMEM(trial_modes.shape, jnp.bfloat16),
            dma((4,)),
            dma((31 * PIECES,)),
            dma((15, PIECES)),
            dma((16, PIECES)),
            dma((3,)),
            dma((3,)),
            dma((3,)),
            dma((3,)),
            dma((31 + 1,)),
            dma((32,)),
        ],
        compiler_params=pltpu.CompilerParams(collective_id=0, has_side_effects=True),
        name="project",
    )(element_tiles, element_blocks, mode_shapes, trial_modes)


def solution(mesh):
    every = P(("sub", "elem"), None)
    return jax.shard_map(
        body,
        mesh=mesh,
        in_specs=(P(("sub", "elem"), None, None), every, every, P("sub", None)),
        out_specs=(every, every),
        check_vma=False,
    )
```

```python
import jax
import jax.numpy as jnp
from jax import lax
from jax.experimental import pallas as pl
from jax.experimental.pallas import tpu as pltpu
from jax.sharding import PartitionSpec as P

MESH = pl.DeviceIdType.MESH
NZ = 8
PIECES = 2
DEPTH = 4
CROSS = ((1, 0),)
SENDS = 31 * PIECES


def kernel(tiles, blocks, modes, trial, reduced, forces, pbuf, turned, tbuf, ids, stiff, part, going, coming, last, in_parts, tr,
           own_sem, p_send, p_recv, s_recv, t_send, t_recv, i_send, i_recv, g_send, g_recv, l_send, r_send, r_recv):
    e = lax.axis_index("elem")
    c = lax.rem(e, 2)
    xh = lax.rem(e // 2, 2)
    z = e // 4
    q = lax.rem(e, 4)
    rows = modes.shape[0] // PIECES
    per = tiles.shape[0]
    wide = stiff.shape[1]
    half = last.shape[1] // 2
    sign = [(1 - 2 * c) * (1 - 2 * (p % 2)) for p in range(PIECES)]

    def level(dz):
        return lax.rem(z + dz + 2 * NZ, NZ)

    def rank(dz, other_x=False, other_c=False):
        return level(dz) * 4 + 2 * (1 - xh if other_x else xh) + (1 - c if other_c else c)

    keep_i = pltpu.make_async_copy(blocks, ids.at[0], own_sem.at[2])
    keep_i.start()
    across, beside = rank(0, True), rank(0, False, True)
    barrier = pltpu.get_barrier_semaphore()
    for device in (rank(1), rank(-1), across, beside):
        pl.semaphore_signal(barrier, inc=1, device_id={"elem": device}, device_id_type=MESH)
    pl.semaphore_wait(barrier, 4)

    waits = []

    def put(src, dst, send, recv, device):
        copy = pltpu.make_async_remote_copy(
            src_ref=src, dst_ref=dst, send_sem=send, recv_sem=recv, device_id={"elem": device}, device_id_type=MESH
        )
        copy.start()
        waits.append(copy)

    def landed(ref, sem):
        pltpu.make_async_copy(ref, ref, sem).wait()

    first = {"A": -1, "B": 3, "C": 7, "D": 11}

    def block_of(kind, j, p, mine=True):
        turn = sign[p] if mine else -sign[p]
        dz = -j * turn if kind in "AC" else j * turn
        return rank(dz, kind in "CD", not mine)

    def piece_of(block, p):
        return pbuf.at[block, pl.ds(p * rows, rows)]

    counter = [0]

    def send_piece(src, block, p, device, recv):
        put(src, piece_of(block, p), p_send.at[counter[0]], recv, device)
        counter[0] += 1

    def forward(kind, j, p):
        block = block_of(kind, j, p)
        slot = first[kind] + j
        src = piece_of(block, p)
        landed(src, p_recv.at[slot, p])
        if (kind == "A" and j < 4) or (kind == "C" and j < 4 and (j + 1, p) not in CROSS):
            send_piece(src, block, p, rank(sign[p]), p_recv.at[slot + 1, p])
        if kind == "A" and (j, p) in CROSS:
            send_piece(src, block, p, across, p_recv.at[first["C"] + j, p])
        if kind == "B":
            if j < 3:
                send_piece(src, block, p, rank(-sign[p]), p_recv.at[slot + 1, p])
            send_piece(src, block, p, across, p_recv.at[first["D"] + j, p])
        send_piece(src, block, p, beside, s_recv.at[slot, p])

    backlog = []

    def turn_over(count):
        for _ in range(min(count, len(backlog))):
            block = backlog.pop(0)
            turned[block] = pbuf[block].T

    cols = pl.ds(pl.multiple_of(q * wide, wide), wide)
    keep = pltpu.make_async_copy(modes, pbuf.at[e], own_sem.at[0])
    keep.start()
    for p in range(PIECES):
        src = modes.at[pl.ds(p * rows, rows)]
        send_piece(src, e, p, rank(sign[p]), p_recv.at[first["A"] + 1, p])
        send_piece(src, e, p, across, p_recv.at[first["C"], p])
    for p in range(PIECES):
        src = modes.at[pl.ds(p * rows, rows)]
        send_piece(src, e, p, rank(-sign[p]), p_recv.at[first["B"] + 1, p])
    for p in range(PIECES):
        send_piece(modes.at[pl.ds(p * rows, rows)], e, p, beside, s_recv.at[15, p])
    keep_i.wait()
    put(ids.at[0], ids.at[1], i_send.at[0], i_recv.at[0], beside)
    put(tiles, tbuf.at[1], t_send.at[0], t_recv.at[0], beside)
    keep_t = pltpu.make_async_copy(tiles, tbuf.at[0], own_sem.at[1])
    keep_t.start()
    keep_r = pltpu.make_async_copy(trial, tr, own_sem.at[3])
    keep_r.start()

    def in_round(r):
        kinds = []
        if r < 4:
            kinds.append(("A", r + 1))
        if r < 3:
            kinds.append(("B", r + 1))
        kinds.append(("C", r))
        if 1 <= r <= 3:
            kinds.append(("D", r))
        return kinds

    def done_in(r, mine):
        if r < 3:
            near = [r + 1, -(r + 1)]
        else:
            near = [4] if r == 3 else []
        far = {0: [0], 4: [4]}.get(r, [r, -r])
        return [rank(d, False, not mine) for d in near] + [rank(d, True, not mine) for d in far]

    def from_beside(r):
        for kind, j in in_round(r):
            for p in range(PIECES):
                landed(piece_of(block_of(kind, j, p, False), p), s_recv.at[first[kind] + j, p])
        backlog.extend(done_in(r, False))

    for r in range(5):
        for kind, j in in_round(r):
            for p in range(PIECES):
                forward(kind, j, p)
                turn_over(3 if r == 4 else 2)
        if r == 1:
            put(tiles, tbuf.at[2], t_send.at[1], t_recv.at[1], across)
            put(ids.at[0], ids.at[2], i_send.at[1], i_recv.at[1], across)
        if r == 3:
            landed(tbuf.at[2], t_recv.at[1])
            put(tbuf.at[2], tbuf.at[3], t_send.at[2], t_recv.at[2], beside)
            landed(ids.at[2], i_recv.at[1])
            put(ids.at[2], ids.at[3], i_send.at[2], i_recv.at[2], beside)
        backlog.extend(done_in(r, True))
        if r == 0:
            keep.wait()
            backlog.append(e)
            for p in range(PIECES):
                landed(piece_of(rank(0, False, True), p), s_recv.at[15, p])
            backlog.append(beside)
            keep_t.wait()
        else:
            from_beside(r - 1)
    landed(tbuf.at[1], t_recv.at[0])
    landed(ids.at[1], i_recv.at[0])
    landed(tbuf.at[3], t_recv.at[2])
    landed(ids.at[3], i_recv.at[2])
    from_beside(4)
    turn_over(len(backlog))

    for g in range(4):
        for i in range(per):
            got = jnp.dot(tbuf[g, i], pbuf[ids[g, 1, i], :, cols], preferred_element_type=jnp.float32)
            k = g * per + i
            stiff[k * 128 : (k + 1) * 128, :] = got.astype(jnp.bfloat16)

    def parts_for(*pairs):
        spans = [pl.ds(pl.multiple_of(m * 256, 256), 256) for m in pairs]
        accs = [jnp.zeros((256, wide), jnp.float32) for _ in pairs]
        for k in range(0, 4 * per, DEPTH):
            which = [ids[n // per, 0, n % per] for n in range(k, k + DEPTH)]
            for n, span in enumerate(spans):
                some = jnp.concatenate([turned[b, span, :] for b in which], axis=1)
                accs[n] += jnp.dot(some, stiff[k * 128 : (k + DEPTH) * 128, :], preferred_element_type=jnp.float32)
        for n, span in enumerate(spans):
            part[span, :] = accs[n]

    def mine(dz, h):
        return part[pl.ds(pl.multiple_of(level(dz) * 2 * half + h * half, half), half), :]

    def step_on(way, step, h, value):
        going[way, step, h] = value.astype(jnp.bfloat16)
        n = (way * 2 + step) * 2 + h
        put(going.at[way, step, h], coming.at[way, step, h], g_send.at[n], g_recv.at[n], rank(1 - 2 * way))

    def come(way, step, h):
        landed(coming.at[way, step, h], g_recv.at[(way * 2 + step) * 2 + h])
        return coming[way, step, h].astype(jnp.float32)

    def rows_at(dz):
        return part[pl.ds(pl.multiple_of(level(dz) * 2 * half, half), 2 * half), :].astype(jnp.bfloat16)

    opposite = lax.rem(z // 2 + 2, 4)
    aside = 2 * lax.rem(z, 2) - 1
    parts_for(opposite, lax.rem(opposite + aside + 4, 4))
    order = (1 - xh, xh)
    for h in order:
        for way in range(2):
            step_on(way, 0, h, mine(3 - 6 * way, h))
    last[3] = rows_at(4)
    for k in range(4):
        put(last.at[3, pl.ds(k * 32, 32)], in_parts.at[12 + q], l_send.at[3 + k], r_recv.at[12 + q], level(4) * 4 + k)
    parts_for(lax.rem(opposite - aside + 4, 4), z // 2)
    last[2] = rows_at(0)
    for k in range(1, 4):
        other = lax.rem(q + k, 4)
        put(last.at[2, pl.ds(pl.multiple_of(other * 32, 32), 32)], in_parts.at[8 + q], l_send.at[k - 1], r_recv.at[8 + q], z * 4 + other)
    in_parts[8 + q] = last[2, pl.ds(pl.multiple_of(q * 32, 32), 32), :]
    for h in order:
        for way in range(2):
            step_on(way, 1, h, come(way, 0, h) + mine(2 - 4 * way, h))
    for h in order:
        for way in range(2):
            dz = 1 - 2 * way
            last[way, pl.ds(pl.multiple_of(h * half, half), half), :] = (come(way, 1, h) + mine(dz, h)).astype(jnp.bfloat16)
            for k in range(2):
                other = 2 * h + k
                put(
                    last.at[way, pl.ds(pl.multiple_of(other * 32, 32), 32)], in_parts.at[way * 4 + q],
                    r_send.at[way * 4 + other], r_recv.at[way * 4 + q], level(dz) * 4 + other,
                )
    for k in range(1, 4):
        other = lax.rem(q + k, 4)
        landed(in_parts.at[8 + other], r_recv.at[8 + other])
    for n in range(4):
        landed(in_parts.at[12 + n], r_recv.at[12 + n])
    for n in range(8):
        landed(in_parts.at[n], r_recv.at[n])
    for quarter in range(4):
        total = in_parts[8 + quarter].astype(jnp.float32) + in_parts[12 + quarter].astype(jnp.float32)
        total += in_parts[quarter].astype(jnp.float32) + in_parts[4 + quarter].astype(jnp.float32)
        reduced[:, quarter * wide : (quarter + 1) * wide] = total
    keep_r.wait()
    high = reduced[...].astype(jnp.bfloat16)
    rest = reduced[...] - high.astype(jnp.float32)
    middle = rest.astype(jnp.bfloat16)
    low = (rest - middle.astype(jnp.float32)).astype(jnp.bfloat16)
    terms = jnp.dot(jnp.concatenate([high, middle, low], axis=0), tr[...], preferred_element_type=jnp.float32)
    own = reduced.shape[0]
    forces[...] = terms[:own] + (terms[own : 2 * own] + terms[2 * own :])
    for copy in waits:
        copy.wait_send()


def body(element_tiles, element_blocks, mode_shapes, trial_modes):
    block, count = mode_shapes.shape
    per = element_tiles.shape[0]
    wide = count // 4
    own = count // 32
    outside = pl.BlockSpec(memory_space=pltpu.HBM)
    in_vmem = pl.BlockSpec(memory_space=pltpu.VMEM)
    dma = pltpu.SemaphoreType.DMA
    narrow, full = jnp.bfloat16, jnp.float32
    return pl.pallas_call(
        kernel,
        out_shape=(
            jax.ShapeDtypeStruct((own, count), full),
            jax.ShapeDtypeStruct((own, trial_modes.shape[1]), full),
        ),
        in_specs=[outside] * 4,
        out_specs=(in_vmem, in_vmem),
        scratch_shapes=[
            pltpu.VMEM((NZ * 4, block, count), narrow),
            pltpu.VMEM((NZ * 4, count, block), narrow),
            pltpu.VMEM((4, per, block, block), narrow),
            pltpu.SMEM((4, 2, per), jnp.int32),
            pltpu.VMEM((4 * per * block, wide), narrow),
            pltpu.VMEM((count, wide), full),
            pltpu.VMEM((2, 2, 2, 2 * own, wide), narrow),
            pltpu.VMEM((2, 2, 2, 2 * own, wide), narrow),
            pltpu.VMEM((4, 4 * own, wide), narrow),
            pltpu.VMEM((16, own, wide), narrow),
            pltpu.VMEM(trial_modes.shape, narrow),
            dma((4,)),
            dma((SENDS,)),
            dma((15, PIECES)),
            dma((16, PIECES)),
            dma((3,)),
            dma((3,)),
            dma((3,)),
            dma((3,)),
            dma((8,)),
            dma((8,)),
            dma((7,)),
            dma((8,)),
            dma((16,)),
        ],
        compiler_params=pltpu.CompilerParams(collective_id=0, has_side_effects=True, vmem_limit_bytes=56360960),
        name="project",
    )(element_tiles, element_blocks.T, mode_shapes, trial_modes)


def solution(mesh):
    every = P(("sub", "elem"), None)
    return jax.shard_map(
        body,
        mesh=mesh,
        in_specs=(P(("sub", "elem"), None, None), every, every, P("sub", None)),
        out_specs=(every, every),
        check_vma=False,
    )
```

```python
import jax
import jax.numpy as jnp
from jax import lax
from jax.experimental import pallas as pl
from jax.experimental.pallas import tpu as pltpu
from jax.sharding import PartitionSpec as P

MESH = pl.DeviceIdType.MESH
NZ = 8
PIECES = 2
DEPTH = 4
CROSS = ((1, 0),)
SENDS = 31 * PIECES


def kernel(tiles, blocks, modes, trial, reduced, forces, pbuf, turned, tbuf, ids, stiff, part, going, coming, last, in_parts, tr,
           own_sem, p_send, p_recv, s_recv, t_send, t_recv, i_send, i_recv, g_send, g_recv, l_send, r_send, r_recv):
    e = lax.axis_index("elem")
    c = lax.rem(e, 2)
    xh = lax.rem(e // 2, 2)
    z = e // 4
    q = lax.rem(e, 4)
    rows = modes.shape[0] // PIECES
    per = tiles.shape[0]
    wide = stiff.shape[1]
    half = last.shape[1] // 2
    sign = [(1 - 2 * c) * (1 - 2 * (p % 2)) for p in range(PIECES)]

    def level(dz):
        return lax.rem(z + dz + 2 * NZ, NZ)

    def rank(dz, other_x=False, other_c=False):
        return level(dz) * 4 + 2 * (1 - xh if other_x else xh) + (1 - c if other_c else c)

    keep_i = pltpu.make_async_copy(blocks, ids.at[0], own_sem.at[2])
    keep_i.start()
    across, beside = rank(0, True), rank(0, False, True)
    barrier = pltpu.get_barrier_semaphore()
    for device in (rank(1), rank(-1), across, beside):
        pl.semaphore_signal(barrier, inc=1, device_id={"elem": device}, device_id_type=MESH)
    pl.semaphore_wait(barrier, 4)

    waits = []

    def put(src, dst, send, recv, device):
        copy = pltpu.make_async_remote_copy(
            src_ref=src, dst_ref=dst, send_sem=send, recv_sem=recv, device_id={"elem": device}, device_id_type=MESH
        )
        copy.start()
        waits.append(copy)

    def landed(ref, sem):
        pltpu.make_async_copy(ref, ref, sem).wait()

    first = {"A": -1, "B": 3, "C": 7, "D": 11}

    def block_of(kind, j, p, mine=True):
        turn = sign[p] if mine else -sign[p]
        dz = -j * turn if kind in "AC" else j * turn
        return rank(dz, kind in "CD", not mine)

    def piece_of(block, p):
        return pbuf.at[block, pl.ds(p * rows, rows)]

    counter = [0]

    def send_piece(src, block, p, device, recv):
        put(src, piece_of(block, p), p_send.at[counter[0]], recv, device)
        counter[0] += 1

    def forward(kind, j, p):
        block = block_of(kind, j, p)
        slot = first[kind] + j
        src = piece_of(block, p)
        landed(src, p_recv.at[slot, p])
        if (kind == "A" and j < 4) or (kind == "C" and j < 4 and (j + 1, p) not in CROSS):
            send_piece(src, block, p, rank(sign[p]), p_recv.at[slot + 1, p])
        if kind == "A" and (j, p) in CROSS:
            send_piece(src, block, p, across, p_recv.at[first["C"] + j, p])
        if kind == "B":
            if j < 3:
                send_piece(src, block, p, rank(-sign[p]), p_recv.at[slot + 1, p])
            send_piece(src, block, p, across, p_recv.at[first["D"] + j, p])
        send_piece(src, block, p, beside, s_recv.at[slot, p])

    backlog = []

    def turn_over(count):
        for _ in range(min(count, len(backlog))):
            block = backlog.pop(0)
            turned[block] = pbuf[block].T

    cols = pl.ds(pl.multiple_of(q * wide, wide), wide)
    keep = pltpu.make_async_copy(modes, pbuf.at[e], own_sem.at[0])
    keep.start()
    for p in range(PIECES):
        src = modes.at[pl.ds(p * rows, rows)]
        send_piece(src, e, p, rank(sign[p]), p_recv.at[first["A"] + 1, p])
        send_piece(src, e, p, across, p_recv.at[first["C"], p])
    for p in range(PIECES):
        src = modes.at[pl.ds(p * rows, rows)]
        send_piece(src, e, p, rank(-sign[p]), p_recv.at[first["B"] + 1, p])
    for p in range(PIECES):
        send_piece(modes.at[pl.ds(p * rows, rows)], e, p, beside, s_recv.at[15, p])
    keep_i.wait()
    put(ids.at[0], ids.at[1], i_send.at[0], i_recv.at[0], beside)
    put(tiles, tbuf.at[1], t_send.at[0], t_recv.at[0], beside)
    keep_t = pltpu.make_async_copy(tiles, tbuf.at[0], own_sem.at[1])
    keep_t.start()
    keep_r = pltpu.make_async_copy(trial, tr, own_sem.at[3])
    keep_r.start()

    def in_round(r):
        kinds = []
        if r < 4:
            kinds.append(("A", r + 1))
        if r < 3:
            kinds.append(("B", r + 1))
        kinds.append(("C", r))
        if 1 <= r <= 3:
            kinds.append(("D", r))
        return kinds

    def done_in(r, mine):
        if r < 3:
            near = [r + 1, -(r + 1)]
        else:
            near = [4] if r == 3 else []
        far = {0: [0], 4: [4]}.get(r, [r, -r])
        return [rank(d, False, not mine) for d in near] + [rank(d, True, not mine) for d in far]

    def from_beside(r):
        for kind, j in in_round(r):
            for p in range(PIECES):
                landed(piece_of(block_of(kind, j, p, False), p), s_recv.at[first[kind] + j, p])
        backlog.extend(done_in(r, False))

    for r in range(5):
        for kind, j in in_round(r):
            for p in range(PIECES):
                forward(kind, j, p)
                turn_over(3 if r == 4 else 2)
        if r == 1:
            put(tiles, tbuf.at[2], t_send.at[1], t_recv.at[1], across)
            put(ids.at[0], ids.at[2], i_send.at[1], i_recv.at[1], across)
        if r == 3:
            landed(tbuf.at[2], t_recv.at[1])
            put(tbuf.at[2], tbuf.at[3], t_send.at[2], t_recv.at[2], beside)
            landed(ids.at[2], i_recv.at[1])
            put(ids.at[2], ids.at[3], i_send.at[2], i_recv.at[2], beside)
        backlog.extend(done_in(r, True))
        if r == 0:
            keep.wait()
            backlog.append(e)
            for p in range(PIECES):
                landed(piece_of(rank(0, False, True), p), s_recv.at[15, p])
            backlog.append(beside)
            keep_t.wait()
        else:
            from_beside(r - 1)
    landed(tbuf.at[1], t_recv.at[0])
    landed(ids.at[1], i_recv.at[0])
    landed(tbuf.at[3], t_recv.at[2])
    landed(ids.at[3], i_recv.at[2])
    from_beside(4)

    for g in range(4):
        for i in range(per):
            got = jnp.dot(tbuf[g, i], pbuf[ids[g, 1, i], :, cols], preferred_element_type=jnp.float32)
            k = g * per + i
            stiff[k * 128 : (k + 1) * 128, :] = got.astype(jnp.bfloat16)
            if i % 2:
                turn_over(1)

    turn_over(len(backlog))

    def parts_for(*pairs):
        spans = [pl.ds(pl.multiple_of(m * 256, 256), 256) for m in pairs]
        accs = [jnp.zeros((256, wide), jnp.float32) for _ in pairs]
        for k in range(0, 4 * per, DEPTH):
            which = [ids[n // per, 0, n % per] for n in range(k, k + DEPTH)]
            for n, span in enumerate(spans):
                some = jnp.concatenate([turned[b, span, :] for b in which], axis=1)
                accs[n] += jnp.dot(some, stiff[k * 128 : (k + DEPTH) * 128, :], preferred_element_type=jnp.float32)
        for n, span in enumerate(spans):
            part[span, :] = accs[n]

    def mine(dz, h):
        return part[pl.ds(pl.multiple_of(level(dz) * 2 * half + h * half, half), half), :]

    def step_on(way, step, h, value):
        going[way, step, h] = value.astype(jnp.bfloat16)
        n = (way * 2 + step) * 2 + h
        put(going.at[way, step, h], coming.at[way, step, h], g_send.at[n], g_recv.at[n], rank(1 - 2 * way))

    def come(way, step, h):
        landed(coming.at[way, step, h], g_recv.at[(way * 2 + step) * 2 + h])
        return coming[way, step, h].astype(jnp.float32)

    def rows_at(dz):
        return part[pl.ds(pl.multiple_of(level(dz) * 2 * half, half), 2 * half), :].astype(jnp.bfloat16)

    opposite = lax.rem(z // 2 + 2, 4)
    aside = 2 * lax.rem(z, 2) - 1
    parts_for(opposite, lax.rem(opposite + aside + 4, 4))
    order = (1 - xh, xh)
    for h in order:
        for way in range(2):
            step_on(way, 0, h, mine(3 - 6 * way, h))
    last[3] = rows_at(4)
    for k in range(4):
        put(last.at[3, pl.ds(k * 32, 32)], in_parts.at[12 + q], l_send.at[3 + k], r_recv.at[12 + q], level(4) * 4 + k)
    parts_for(lax.rem(opposite - aside + 4, 4), z // 2)
    last[2] = rows_at(0)
    for k in range(1, 4):
        other = lax.rem(q + k, 4)
        put(last.at[2, pl.ds(pl.multiple_of(other * 32, 32), 32)], in_parts.at[8 + q], l_send.at[k - 1], r_recv.at[8 + q], z * 4 + other)
    in_parts[8 + q] = last[2, pl.ds(pl.multiple_of(q * 32, 32), 32), :]
    for h in order:
        for way in range(2):
            step_on(way, 1, h, come(way, 0, h) + mine(2 - 4 * way, h))
    for h in order:
        for way in range(2):
            dz = 1 - 2 * way
            last[way, pl.ds(pl.multiple_of(h * half, half), half), :] = (come(way, 1, h) + mine(dz, h)).astype(jnp.bfloat16)
            for k in range(2):
                other = 2 * h + k
                put(
                    last.at[way, pl.ds(pl.multiple_of(other * 32, 32), 32)], in_parts.at[way * 4 + q],
                    r_send.at[way * 4 + other], r_recv.at[way * 4 + q], level(dz) * 4 + other,
                )
    for k in range(1, 4):
        other = lax.rem(q + k, 4)
        landed(in_parts.at[8 + other], r_recv.at[8 + other])
    for n in range(4):
        landed(in_parts.at[12 + n], r_recv.at[12 + n])
    for n in range(8):
        landed(in_parts.at[n], r_recv.at[n])
    for quarter in range(4):
        total = in_parts[8 + quarter].astype(jnp.float32) + in_parts[12 + quarter].astype(jnp.float32)
        total += in_parts[quarter].astype(jnp.float32) + in_parts[4 + quarter].astype(jnp.float32)
        reduced[:, quarter * wide : (quarter + 1) * wide] = total
    keep_r.wait()
    high = reduced[...].astype(jnp.bfloat16)
    rest = reduced[...] - high.astype(jnp.float32)
    middle = rest.astype(jnp.bfloat16)
    low = (rest - middle.astype(jnp.float32)).astype(jnp.bfloat16)
    terms = jnp.dot(jnp.concatenate([high, middle, low], axis=0), tr[...], preferred_element_type=jnp.float32)
    own = reduced.shape[0]
    forces[...] = terms[:own] + (terms[own : 2 * own] + terms[2 * own :])
    for copy in waits:
        copy.wait_send()


def body(element_tiles, element_blocks, mode_shapes, trial_modes):
    block, count = mode_shapes.shape
    per = element_tiles.shape[0]
    wide = count // 4
    own = count // 32
    outside = pl.BlockSpec(memory_space=pltpu.HBM)
    in_vmem = pl.BlockSpec(memory_space=pltpu.VMEM)
    dma = pltpu.SemaphoreType.DMA
    narrow, full = jnp.bfloat16, jnp.float32
    return pl.pallas_call(
        kernel,
        out_shape=(
            jax.ShapeDtypeStruct((own, count), full),
            jax.ShapeDtypeStruct((own, trial_modes.shape[1]), full),
        ),
        in_specs=[outside] * 4,
        out_specs=(in_vmem, in_vmem),
        scratch_shapes=[
            pltpu.VMEM((NZ * 4, block, count), narrow),
            pltpu.VMEM((NZ * 4, count, block), narrow),
            pltpu.VMEM((4, per, block, block), narrow),
            pltpu.SMEM((4, 2, per), jnp.int32),
            pltpu.VMEM((4 * per * block, wide), narrow),
            pltpu.VMEM((count, wide), full),
            pltpu.VMEM((2, 2, 2, 2 * own, wide), narrow),
            pltpu.VMEM((2, 2, 2, 2 * own, wide), narrow),
            pltpu.VMEM((4, 4 * own, wide), narrow),
            pltpu.VMEM((16, own, wide), narrow),
            pltpu.VMEM(trial_modes.shape, narrow),
            dma((4,)),
            dma((SENDS,)),
            dma((15, PIECES)),
            dma((16, PIECES)),
            dma((3,)),
            dma((3,)),
            dma((3,)),
            dma((3,)),
            dma((8,)),
            dma((8,)),
            dma((7,)),
            dma((8,)),
            dma((16,)),
        ],
        compiler_params=pltpu.CompilerParams(collective_id=0, has_side_effects=True, vmem_limit_bytes=56360960),
        name="project",
    )(element_tiles, element_blocks.T, mode_shapes, trial_modes)


def solution(mesh):
    every = P(("sub", "elem"), None)
    return jax.shard_map(
        body,
        mesh=mesh,
        in_specs=(P(("sub", "elem"), None, None), every, every, P("sub", None)),
        out_specs=(every, every),
        check_vma=False,
    )
```
